32 devices in a mesh: grp: 2 (over y), row: 4 (over x, core), col: 4 (over z).
Axes of the slice: x: 2, y: 2, z: 4, core: 2. Of those that a mesh axis runs over, the one named last changes fastest.
Arguments:
- amplitudes: bfloat16 [32768, 16384], P(('grp', 'row'), 'col'), parts along dimension 0, may hold values from -0.046875 to 0.046875
- cholesky: bfloat16 [1024, 32768], P('row', ('grp', 'col')), parts along dimension 1, may hold values from -1.078125 to 1.078125
- occ_index: int32 [32768], P('grp'), parts along dimension 0, may hold values from 0 to 31
- vir_index: int32 [32768], P('grp'), parts along dimension 0, may hold values from 0 to 511
- eps_occ: float32 [64], P('grp'), parts along dimension 0, may hold values from -2 to -0.3
- eps_vir: float32 [1024], P('grp'), parts along dimension 0, may hold values from 0.2 to 3
Outputs:
- new_amplitudes: bfloat16 [32768, 16384], P(('grp', 'row'), 'col'), parts along dimension 0
The draws below stay inside these ranges and needn't reach their ends.
There are 2 independent parts, one for each index of `grp`. The reference program is written for one: setup_inputs(seed, part) draws one part's arguments, and reference() takes and returns one part's arrays. A program takes and returns all parts, laid end to end along the dimension named above; each array names one. Nothing has to cross between parts.
All inputs are finite; a program needn't handle non-finite values.
Results may differ from the reference program's by a relative error of at most 0.0056.
Values may be sent and summed in bfloat16 or wider, within the bound.
A program may use at most 128 MiB of HBM per device.

```python
import math
import jax
import jax.numpy as jnp
from jax import lax

NOCC = 32
NVIR = 512
NAUX = 1024
P_SIZE = 16384


def place_ends(drawn, own_key, least, largest):
    dims = drawn.shape
    index_at = [jax.random.randint(jax.random.fold_in(own_key, axis), (), 0, dims[axis]) for axis in range(len(dims))]
    drawn = drawn.at[tuple(index_at)].set(least)
    longest = dims.index(max(dims))
    index_at[longest] = (index_at[longest] + 1) % dims[longest]
    return drawn.at[tuple(index_at)].set(largest)


def steps_of(stream_key, shape, pieces, least, top_value):
    factor_of, own = 1.0, jax.random.fold_in(stream_key, 6)
    for axis_at, parts in pieces:
        heights = jnp.exp(jax.random.uniform(jax.random.fold_in(own, axis_at), (parts,), jnp.float32, least / len(pieces), top_value / len(pieces)))
        factor_of = factor_of * jnp.repeat(heights, shape[axis_at] // parts).reshape([-1 if axis == axis_at else 1 for axis in range(len(shape))])
    return factor_of


def gaussian(rng, extent, scale, limit, shards=(), kind=jnp.bfloat16):
    entries = scale * jax.random.normal(rng, extent, jnp.float32)
    if shards:
        entries = entries * steps_of(rng, extent, shards, -0.22, 0.18)
    return jnp.clip(entries, -limit, limit).astype(kind)


def setup_inputs(seed: int = 0, part: int = 0) -> dict:
    splits = jax.random.split(jax.random.key(seed), 7)
    part_splits = jax.random.split(jax.random.fold_in(splits[6], part), 7)
    return {
        "amplitudes": gaussian(part_splits[0], (P_SIZE, P_SIZE), P_SIZE ** -0.5, 0.046875, ((0, 4), (1, 4))),
        "cholesky": gaussian(part_splits[1], (NAUX, P_SIZE), 0.18, 1.078125, ((0, 4), (1, 4))),
        "occ_index": place_ends(jax.random.randint(part_splits[2], (P_SIZE,), 0, NOCC), jax.random.fold_in(part_splits[2], 1), 0, NOCC - 1).astype(jnp.int32),
        "vir_index": place_ends(jax.random.randint(part_splits[3], (P_SIZE,), 0, NVIR), jax.random.fold_in(part_splits[3], 1), 0, NVIR - 1).astype(jnp.int32),
        "eps_occ": jnp.clip(jax.random.uniform(part_splits[4], (NOCC,), jnp.float32, -2.0, -0.3), -2.0, -0.3),
        "eps_vir": jnp.clip(jax.random.uniform(part_splits[5], (NVIR,), jnp.float32, 0.2, 3.0), 0.2, 3.0),
    }


def reference(amplitudes, cholesky, occ_index, vir_index, eps_occ, eps_vir):
    gap = eps_vir[vir_index] - eps_occ[occ_index]
    dressed = jnp.dot(cholesky, amplitudes, preferred_element_type=jnp.float32)
    ydress = (cholesky.astype(jnp.float32) + dressed).astype(jnp.bfloat16)
    width = math.gcd(P_SIZE, 1024)

    def gram_block(block_id):
        columns = lax.dynamic_slice_in_dim(ydress, block_id * width, width, 1)
        gram = lax.dot_general(columns, ydress, (((0,), (0,)), ((), ())), preferred_element_type=jnp.float32)
        gaps = lax.dynamic_slice_in_dim(gap, block_id * width, width, 0)
        return (-gram / (gaps[:, None] + gap[None, :])).astype(jnp.bfloat16)

    blocks = lax.map(gram_block, jnp.arange(P_SIZE // width, dtype=jnp.int32))
    return blocks.reshape(P_SIZE, P_SIZE)
```

```python
import functools

import jax
import jax.numpy as jnp
from jax import lax
from jax.experimental import pallas as pl
from jax.experimental.pallas import tpu as pltpu
from jax.sharding import PartitionSpec as P

MESH = pl.DeviceIdType.MESH


def pair_gaps(occ_index, vir_index, eps_occ, eps_vir, begin_pair, pair_count):
    occ_rows = lax.dynamic_slice_in_dim(occ_index, begin_pair, pair_count, 0)
    vir_rows = lax.dynamic_slice_in_dim(vir_index, begin_pair, pair_count, 0)
    occ_table = jnp.arange(eps_occ.shape[0], dtype=jnp.int32)
    vir_table = jnp.arange(eps_vir.shape[0], dtype=jnp.int32)
    occ_energy = jnp.sum(
        jnp.where(occ_rows[:, None] == occ_table[None, :], eps_occ[None, :], 0.0), axis=1
    )
    vir_energy = jnp.sum(
        jnp.where(vir_rows[:, None] == vir_table[None, :], eps_vir[None, :], 0.0), axis=1
    )
    return vir_energy - occ_energy


def enter(row_count, col_count, me_row, me_col):
    barrier = pltpu.get_barrier_semaphore()
    for step in range(1, row_count):
        pl.semaphore_signal(
            barrier,
            inc=1,
            device_id={"row": lax.rem(me_row + step, row_count)},
            device_id_type=MESH,
        )
    for condition, where in ((me_col > 0, -1), (me_col < col_count - 1, 1)):

        @pl.when(condition)
        def _():
            pl.semaphore_signal(
                barrier, inc=1, device_id={"col": me_col + where}, device_id_type=MESH
            )

    neighbours = jnp.minimum(me_col, 1) + jnp.minimum(col_count - 1 - me_col, 1)
    pl.semaphore_wait(barrier, row_count - 1 + neighbours)


class Gather:
    def __init__(self, row_count, col_count, pieces, own, rows, held, sems):
        self.row_count, self.col_count, self.pieces = row_count, col_count, pieces
        self.own, self.rows, self.held = own, rows, held
        (self.load, self.send_line, self.recv_line, self.send_row, self.recv_row, self.keep) = sems
        self.me_row, self.me_col = lax.axis_index("row"), lax.axis_index("col")
        self.depth = own.shape[0] // pieces
        self.share = row_count // col_count
        self.width = own.shape[1] // self.share

    def part(self, piece):
        return pl.ds(piece * self.depth, self.depth)

    def load_copy(self, piece):
        return pltpu.make_async_copy(
            self.own.at[self.part(piece), :],
            self.held.at[self.me_col, self.part(piece), :],
            self.load.at[piece],
        )

    def line_copy(self, side, block, hops, piece):
        ref = self.held.at[block, self.part(piece), :]
        return pltpu.make_async_remote_copy(
            src_ref=ref,
            dst_ref=ref,
            send_sem=self.send_line.at[side, hops, piece],
            recv_sem=self.recv_line.at[side, hops, piece],
            device_id={"col": self.me_col + (1 if side == 0 else -1)},
            device_id_type=MESH,
        )

    def row_copy(self, block, index, piece):
        return pltpu.make_async_remote_copy(
            src_ref=self.held.at[
                block, self.part(piece), pl.ds(index * self.width, self.width)
            ],
            dst_ref=self.rows.at[self.me_row, self.part(piece), :],
            send_sem=self.send_row.at[block, index, piece],
            recv_sem=self.recv_row.at[self.me_row, piece],
            device_id={"row": block * self.share + index},
            device_id_type=MESH,
        )

    def keep_copy(self, block, index, piece):
        return pltpu.make_async_copy(
            self.held.at[block, self.part(piece), pl.ds(index * self.width, self.width)],
            self.rows.at[self.me_row, self.part(piece), :],
            self.keep.at[piece],
        )

    def on(self, side):
        return self.me_col < self.col_count - 1 if side == 0 else self.me_col > 0

    def spread(self, block, piece):
        for index in range(self.share):
            target = block * self.share + index

            @pl.when(target == self.me_row)
            def _():
                self.keep_copy(block, index, piece).start()

            @pl.when(target != self.me_row)
            def _():
                self.row_copy(block, index, piece).start()

    def begin(self, piece):
        self.load_copy(piece).wait()
        for side in range(2):

            @pl.when(self.on(side))
            def _():
                self.line_copy(side, self.me_col, 0, piece).start()

        self.spread(self.me_col, piece)

    def source(self, side, hops):
        block = self.me_col - hops if side == 0 else self.me_col + hops
        exists = self.me_col >= hops if side == 0 else self.me_col + hops < self.col_count
        return block, exists

    def arrive(self, hops, piece):
        for side in range(2):
            block, exists = self.source(side, hops)

            @pl.when(exists)
            def _():
                self.line_copy(side, block, hops - 1, piece).wait_recv()

                if hops < self.col_count - 1:

                    @pl.when(self.on(side))
                    def _():
                        self.line_copy(side, block, hops, piece).start()

                self.spread(block, piece)

    def wait_rows(self, piece):
        for other in range(self.row_count):

            @pl.when(other != self.me_row)
            def _():
                pltpu.make_async_remote_copy(
                    src_ref=self.rows.at[other, self.part(piece), :],
                    dst_ref=self.rows.at[other, self.part(piece), :],
                    send_sem=self.send_row.at[0, 0, piece],
                    recv_sem=self.recv_row.at[other, piece],
                    device_id={"row": other},
                    device_id_type=MESH,
                ).wait_recv()

        for block in range(self.col_count):
            for index in range(self.share):

                @pl.when(block * self.share + index == self.me_row)
                def _():
                    self.keep_copy(block, index, piece).wait()

    def wait_sends(self, piece):
        for side in range(2):
            for hops in range(self.col_count - 1):
                block, exists = self.source(side, hops)

                @pl.when(jnp.logical_and(exists, self.on(side)))
                def _():
                    self.line_copy(side, block, hops, piece).wait_send()

        for block in range(self.col_count):
            for index in range(self.share):

                @pl.when(block * self.share + index != self.me_row)
                def _():
                    self.row_copy(block, index, piece).wait_send()


def gather_sems(row_count, col_count, pieces):
    return [
        pltpu.SemaphoreType.DMA((pieces,)),
        pltpu.SemaphoreType.DMA((2, col_count, pieces)),
        pltpu.SemaphoreType.DMA((2, col_count, pieces)),
        pltpu.SemaphoreType.DMA((col_count, row_count // col_count, pieces)),
        pltpu.SemaphoreType.DMA((row_count, pieces)),
        pltpu.SemaphoreType.DMA((pieces,)),
    ]


class Columns:
    def __init__(self, row_count, pieces, own, cols, sems):
        self.row_count, self.pieces, self.own, self.cols = row_count, pieces, own, cols
        self.load, self.send, self.recv, self.send_on = sems
        self.me_row = lax.axis_index("row")
        self.partner = self.me_row + 1 - 2 * lax.rem(self.me_row, 2)
        self.depth = own.shape[0] // pieces

    def part(self, piece):
        return pl.ds(piece * self.depth, self.depth)

    def copy(self, owner, target, sem, piece, src=None):
        dst = self.cols.at[owner, self.part(piece), :]
        return pltpu.make_async_remote_copy(
            src_ref=dst if src is None else src,
            dst_ref=dst,
            send_sem=sem,
            recv_sem=self.recv.at[owner, piece],
            device_id={"row": target},
            device_id_type=MESH,
        )

    def peers(self):
        peers = [(0, self.partner)]
        for step in range(1, self.row_count // 2):
            peers.append((step, lax.rem(self.me_row + 2 * step, self.row_count)))
        return peers

    def first(self, slot, target, piece, src):
        return self.copy(self.me_row, target, self.send.at[slot, piece], piece, src)

    def begin(self, piece, src):
        for slot, target in self.peers():
            self.first(slot, target, piece, src).start()

    def arrive(self, piece):
        for slot, owner in self.peers()[1:]:
            self.copy(owner, self.partner, self.send_on.at[slot, piece], piece).wait_recv()
            self.copy(owner, self.partner, self.send_on.at[slot, piece], piece).start()

    def finish(self, piece, src):
        for slot, target in self.peers():
            self.first(slot, target, piece, src).wait_send()
        self.copy(self.partner, self.partner, self.send.at[0, piece], piece).wait_recv()
        for slot, owner in self.peers()[1:]:
            self.copy(owner, self.partner, self.send_on.at[slot, piece], piece).wait_send()
            theirs = lax.rem(self.partner + 2 * slot, self.row_count)
            self.copy(theirs, self.partner, self.send.at[0, piece], piece).wait_recv()


def columns_sems(row_count, pieces):
    return [
        pltpu.SemaphoreType.DMA((pieces,)),
        pltpu.SemaphoreType.DMA((row_count // 2, pieces)),
        pltpu.SemaphoreType.DMA((row_count, pieces)),
        pltpu.SemaphoreType.DMA((row_count // 2, pieces)),
    ]


def gather_kernel(row_count, col_count, pieces, with_cols, *refs):
    own, rows = refs[0], refs[1]
    rest = refs[2:]
    columns = None
    if with_cols:
        cols, held = rest[0], rest[1]
        sems, cols_sems = rest[2:8], rest[8:12]
        columns = Columns(row_count, pieces, own, cols, cols_sems)
    else:
        held, sems = rest[0], rest[1:7]
    gather = Gather(row_count, col_count, pieces, own, rows, held, sems)
    for piece in range(pieces):
        gather.load_copy(piece).start()
    enter(row_count, col_count, gather.me_row, gather.me_col)

    def source(piece):
        return held.at[gather.me_col, gather.part(piece), :]

    def own_cols(piece):
        return pltpu.make_async_copy(
            source(piece), cols.at[gather.me_row, gather.part(piece), :], columns.load.at[piece]
        )

    def begin(piece):
        gather.begin(piece)
        if with_cols:
            own_cols(piece).start()
            columns.begin(piece, source(piece))

    for piece in range(min(2, pieces)):
        begin(piece)
    for step in range(pieces + col_count - 2):
        if step + 2 < pieces:
            begin(step + 2)
        for hops in range(1, col_count):
            if 0 <= step - hops + 1 < pieces:
                gather.arrive(hops, step - hops + 1)
        if with_cols and step < pieces:
            columns.arrive(step)
    for piece in range(pieces):
        gather.wait_rows(piece)
        gather.wait_sends(piece)
        if with_cols:
            own_cols(piece).wait()
            columns.finish(piece, source(piece))


def gather_pairs(own, row_count, col_count, with_cols, collective_id):
    depth, width = own.shape
    pieces = max(1, min(4, depth // 16))
    rows = jax.ShapeDtypeStruct(
        (row_count, depth, width * col_count // row_count), own.dtype
    )
    cols = jax.ShapeDtypeStruct((row_count, depth, width), own.dtype)
    out_shape = (rows, cols) if with_cols else (rows,)
    scratch = [pltpu.VMEM((col_count, depth, width), own.dtype)]
    scratch += gather_sems(row_count, col_count, pieces)
    if with_cols:
        scratch += columns_sems(row_count, pieces)
    out = pl.pallas_call(
        functools.partial(gather_kernel, row_count, col_count, pieces, with_cols),
        out_shape=out_shape,
        in_specs=[pl.BlockSpec(memory_space=pl.ANY)],
        out_specs=tuple(pl.BlockSpec(memory_space=pl.ANY) for _ in out_shape),
        scratch_shapes=scratch,
        compiler_params=pltpu.CompilerParams(
            collective_id=collective_id, has_side_effects=True
        ),
        name="gather_cols" if with_cols else "gather_rows",
    )(own)
    return [item.reshape(row_count * depth, item.shape[2]) for item in out]


def local(row_count, col_count, amplitudes, cholesky, occ_index, vir_index, eps_occ, eps_vir):
    row_position = lax.axis_index("row")
    col_position = lax.axis_index("col")
    rows_block, cols_block = amplitudes.shape
    (chol_rows,) = gather_pairs(cholesky, row_count, col_count, False, 0)
    dressed = lax.psum_scatter(
        jnp.dot(chol_rows, amplitudes, preferred_element_type=jnp.float32),
        "row",
        scatter_dimension=0,
        tiled=True,
    )
    ydress = (cholesky.astype(jnp.float32) + dressed).astype(jnp.bfloat16)
    contract = (((0,), (0,)), ((), ()))
    ydress_rows, ydress_cols = gather_pairs(ydress, row_count, col_count, True, 1)
    gram = lax.dot_general(
        ydress_rows, ydress_cols, contract, preferred_element_type=jnp.float32
    )
    gap_rows = pair_gaps(
        occ_index, vir_index, eps_occ, eps_vir, row_position * rows_block, rows_block
    )
    gap_cols = pair_gaps(
        occ_index, vir_index, eps_occ, eps_vir, col_position * cols_block, cols_block
    )
    return (-gram / (gap_rows[:, None] + gap_cols[None, :])).astype(jnp.bfloat16)


def solution(mesh):
    return jax.shard_map(
        functools.partial(local, mesh.shape["row"], mesh.shape["col"]),
        mesh=mesh,
        in_specs=(
            P(("grp", "row"), "col"),
            P("row", ("grp", "col")),
            P("grp"),
            P("grp"),
            P("grp"),
            P("grp"),
        ),
        out_specs=P(("grp", "row"), "col"),
        check_vma=False,
    )
```

```python
import functools

import jax
import jax.numpy as jnp
from jax import lax
from jax.experimental import pallas as pl
from jax.experimental.pallas import tpu as pltpu
from jax.sharding import PartitionSpec as P

MESH = pl.DeviceIdType.MESH


def pair_gaps(occ_index, vir_index, eps_occ, eps_vir, begin_pair, pair_count):
    occ_rows = lax.dynamic_slice_in_dim(occ_index, begin_pair, pair_count, 0)
    vir_rows = lax.dynamic_slice_in_dim(vir_index, begin_pair, pair_count, 0)
    occ_table = jnp.arange(eps_occ.shape[0], dtype=jnp.int32)
    vir_table = jnp.arange(eps_vir.shape[0], dtype=jnp.int32)
    occ_energy = jnp.sum(
        jnp.where(occ_rows[:, None] == occ_table[None, :], eps_occ[None, :], 0.0), axis=1
    )
    vir_energy = jnp.sum(
        jnp.where(vir_rows[:, None] == vir_table[None, :], eps_vir[None, :], 0.0), axis=1
    )
    return vir_energy - occ_energy


def enter(row_count, col_count, me_row, me_col):
    barrier = pltpu.get_barrier_semaphore()
    for step in range(1, row_count):
        pl.semaphore_signal(
            barrier,
            inc=1,
            device_id={"row": lax.rem(me_row + step, row_count)},
            device_id_type=MESH,
        )
    for condition, where in ((me_col > 0, -1), (me_col < col_count - 1, 1)):

        @pl.when(condition)
        def _():
            pl.semaphore_signal(
                barrier, inc=1, device_id={"col": me_col + where}, device_id_type=MESH
            )

    neighbours = jnp.minimum(me_col, 1) + jnp.minimum(col_count - 1 - me_col, 1)
    pl.semaphore_wait(barrier, row_count - 1 + neighbours)


class Gather:
    def __init__(self, row_count, col_count, pieces, own, rows, held, sems, direct=False):
        self.direct = direct
        self.row_count, self.col_count, self.pieces = row_count, col_count, pieces
        self.own, self.rows, self.held = own, rows, held
        (self.load, self.send_line, self.recv_line, self.send_row, self.recv_row, self.keep) = sems
        self.me_row, self.me_col = lax.axis_index("row"), lax.axis_index("col")
        self.depth = own.shape[0] // pieces
        self.share = row_count // col_count
        self.width = own.shape[1] // self.share

    def part(self, piece):
        return pl.ds(piece * self.depth, self.depth)

    def load_copy(self, piece):
        return pltpu.make_async_copy(
            self.own.at[self.part(piece), :],
            self.held.at[self.me_col, self.part(piece), :],
            self.load.at[piece],
        )

    def block_ref(self, block, piece, mine):
        if mine and self.direct:
            return self.own.at[self.part(piece), :]
        return self.held.at[block, self.part(piece), :]

    def block_part(self, block, index, piece, mine):
        columns = pl.ds(index * self.width, self.width)
        if mine and self.direct:
            return self.own.at[self.part(piece), columns]
        return self.held.at[block, self.part(piece), columns]

    def row_ref(self, owner, target, piece):
        if not self.direct:
            return self.rows.at[owner, self.part(piece), :]
        half = self.row_count // 2
        other = lax.rem(owner + target, 2)
        base = target + other * (1 - 2 * lax.rem(target, 2))
        slot = lax.rem(owner - base + self.row_count, self.row_count) // 2 + other * half
        begin = pl.multiple_of(slot * self.depth, self.depth)
        return self.rows.at[piece, pl.ds(begin, self.depth), :]

    def line_copy(self, side, block, hops, piece):
        return pltpu.make_async_remote_copy(
            src_ref=self.block_ref(block, piece, hops == 0),
            dst_ref=self.held.at[block, self.part(piece), :],
            send_sem=self.send_line.at[side, hops, piece],
            recv_sem=self.recv_line.at[side, hops, piece],
            device_id={"col": self.me_col + (1 if side == 0 else -1)},
            device_id_type=MESH,
        )

    def row_copy(self, block, index, piece, mine=False):
        return pltpu.make_async_remote_copy(
            src_ref=self.block_part(block, index, piece, mine),
            dst_ref=self.row_ref(self.me_row, block * self.share + index, piece),
            send_sem=self.send_row.at[block, index, piece],
            recv_sem=self.recv_row.at[self.me_row, piece],
            device_id={"row": block * self.share + index},
            device_id_type=MESH,
        )

    def keep_copy(self, block, index, piece, mine=False):
        return pltpu.make_async_copy(
            self.block_part(block, index, piece, mine),
            self.row_ref(self.me_row, self.me_row, piece),
            self.keep.at[piece],
        )

    def on(self, side):
        return self.me_col < self.col_count - 1 if side == 0 else self.me_col > 0

    def spread(self, block, piece, mine=False):
        for index in range(self.share):
            target = block * self.share + index

            @pl.when(target == self.me_row)
            def _():
                self.keep_copy(block, index, piece, mine).start()

            @pl.when(target != self.me_row)
            def _():
                self.row_copy(block, index, piece, mine).start()

    def begin(self, piece):
        if not self.direct:
            self.load_copy(piece).wait()
        for side in range(2):

            @pl.when(self.on(side))
            def _():
                self.line_copy(side, self.me_col, 0, piece).start()

        self.spread(self.me_col, piece, True)

    def source(self, side, hops):
        block = self.me_col - hops if side == 0 else self.me_col + hops
        exists = self.me_col >= hops if side == 0 else self.me_col + hops < self.col_count
        return block, exists

    def arrive(self, hops, piece):
        for side in range(2):
            block, exists = self.source(side, hops)

            @pl.when(exists)
            def _():
                self.line_copy(side, block, hops - 1, piece).wait_recv()

                if hops < self.col_count - 1:

                    @pl.when(self.on(side))
                    def _():
                        self.line_copy(side, block, hops, piece).start()

                self.spread(block, piece)

    def wait_rows(self, piece):
        for other in range(self.row_count):

            @pl.when(other != self.me_row)
            def _():
                pltpu.make_async_remote_copy(
                    src_ref=self.row_ref(other, self.me_row, piece),
                    dst_ref=self.row_ref(other, self.me_row, piece),
                    send_sem=self.send_row.at[0, 0, piece],
                    recv_sem=self.recv_row.at[other, piece],
                    device_id={"row": other},
                    device_id_type=MESH,
                ).wait_recv()

        for block in range(self.col_count):
            for index in range(self.share):

                @pl.when(block * self.share + index == self.me_row)
                def _():
                    self.keep_copy(block, index, piece).wait()

    def wait_sends(self, piece):
        for side in range(2):
            for hops in range(self.col_count - 1):
                block, exists = self.source(side, hops)

                @pl.when(jnp.logical_and(exists, self.on(side)))
                def _():
                    self.line_copy(side, block, hops, piece).wait_send()

        for block in range(self.col_count):
            for index in range(self.share):

                @pl.when(block * self.share + index != self.me_row)
                def _():
                    self.row_copy(block, index, piece).wait_send()


def gather_sems(row_count, col_count, pieces):
    return [
        pltpu.SemaphoreType.DMA((pieces,)),
        pltpu.SemaphoreType.DMA((2, col_count, pieces)),
        pltpu.SemaphoreType.DMA((2, col_count, pieces)),
        pltpu.SemaphoreType.DMA((col_count, row_count // col_count, pieces)),
        pltpu.SemaphoreType.DMA((row_count, pieces)),
        pltpu.SemaphoreType.DMA((pieces,)),
    ]


class Columns:
    def __init__(self, row_count, pieces, own, cols, sems):
        self.row_count, self.pieces, self.own, self.cols = row_count, pieces, own, cols
        self.load, self.send, self.recv, self.send_on = sems
        self.me_row = lax.axis_index("row")
        self.partner = self.me_row + 1 - 2 * lax.rem(self.me_row, 2)
        self.depth = own.shape[0] // pieces

    def part(self, piece):
        return pl.ds(piece * self.depth, self.depth)

    def copy(self, owner, target, sem, piece, src=None):
        dst = self.cols.at[owner, self.part(piece), :]
        return pltpu.make_async_remote_copy(
            src_ref=dst if src is None else src,
            dst_ref=dst,
            send_sem=sem,
            recv_sem=self.recv.at[owner, piece],
            device_id={"row": target},
            device_id_type=MESH,
        )

    def peers(self):
        peers = [(0, self.partner)]
        for step in range(1, self.row_count // 2):
            peers.append((step, lax.rem(self.me_row + 2 * step, self.row_count)))
        return peers

    def first(self, slot, target, piece, src):
        return self.copy(self.me_row, target, self.send.at[slot, piece], piece, src)

    def begin(self, piece, src):
        for slot, target in self.peers():
            self.first(slot, target, piece, src).start()

    def arrive(self, piece):
        for slot, owner in self.peers()[1:]:
            self.copy(owner, self.partner, self.send_on.at[slot, piece], piece).wait_recv()
            self.copy(owner, self.partner, self.send_on.at[slot, piece], piece).start()

    def finish(self, piece, src):
        for slot, target in self.peers():
            self.first(slot, target, piece, src).wait_send()
        self.copy(self.partner, self.partner, self.send.at[0, piece], piece).wait_recv()
        for slot, owner in self.peers()[1:]:
            self.copy(owner, self.partner, self.send_on.at[slot, piece], piece).wait_send()
            theirs = lax.rem(self.partner + 2 * slot, self.row_count)
            self.copy(theirs, self.partner, self.send.at[0, piece], piece).wait_recv()


def columns_sems(row_count, pieces):
    return [
        pltpu.SemaphoreType.DMA((pieces,)),
        pltpu.SemaphoreType.DMA((row_count // 2, pieces)),
        pltpu.SemaphoreType.DMA((row_count, pieces)),
        pltpu.SemaphoreType.DMA((row_count // 2, pieces)),
    ]


def gather_kernel(row_count, col_count, pieces, with_cols, *refs):
    own, rows = refs[0], refs[1]
    rest = refs[2:]
    columns = None
    if with_cols:
        cols, held = rest[0], rest[1]
        sems, cols_sems = rest[2:8], rest[8:12]
        columns = Columns(row_count, pieces, own, cols, cols_sems)
    else:
        held, sems = rest[0], rest[1:7]
    gather = Gather(row_count, col_count, pieces, own, rows, held, sems)
    for piece in range(pieces):
        gather.load_copy(piece).start()
    enter(row_count, col_count, gather.me_row, gather.me_col)

    def source(piece):
        return held.at[gather.me_col, gather.part(piece), :]

    def own_cols(piece):
        return pltpu.make_async_copy(
            source(piece), cols.at[gather.me_row, gather.part(piece), :], columns.load.at[piece]
        )

    def begin(piece):
        gather.begin(piece)
        if with_cols:
            own_cols(piece).start()
            columns.begin(piece, source(piece))

    for piece in range(min(2, pieces)):
        begin(piece)
    for step in range(pieces + col_count - 2):
        if step + 2 < pieces:
            begin(step + 2)
        for hops in range(1, col_count):
            if 0 <= step - hops + 1 < pieces:
                gather.arrive(hops, step - hops + 1)
        if with_cols and step < pieces:
            columns.arrive(step)
    for piece in range(pieces):
        gather.wait_rows(piece)
        gather.wait_sends(piece)
        if with_cols:
            own_cols(piece).wait()
            columns.finish(piece, source(piece))


def gather_pairs(own, row_count, col_count, with_cols, collective_id):
    depth, width = own.shape
    pieces = max(1, min(4, depth // 16))
    rows = jax.ShapeDtypeStruct(
        (row_count, depth, width * col_count // row_count), own.dtype
    )
    cols = jax.ShapeDtypeStruct((row_count, depth, width), own.dtype)
    out_shape = (rows, cols) if with_cols else (rows,)
    scratch = [pltpu.VMEM((col_count, depth, width), own.dtype)]
    scratch += gather_sems(row_count, col_count, pieces)
    if with_cols:
        scratch += columns_sems(row_count, pieces)
    out = pl.pallas_call(
        functools.partial(gather_kernel, row_count, col_count, pieces, with_cols),
        out_shape=out_shape,
        in_specs=[pl.BlockSpec(memory_space=pl.ANY)],
        out_specs=tuple(pl.BlockSpec(memory_space=pl.ANY) for _ in out_shape),
        scratch_shapes=scratch,
        compiler_params=pltpu.CompilerParams(
            collective_id=collective_id, has_side_effects=True
        ),
        name="gather_cols" if with_cols else "gather_rows",
    )(own)
    return [item.reshape(row_count * depth, item.shape[2]) for item in out]


def dress_kernel(
    row_count, col_count, pieces, amplitudes, own, held, dressed, table, rows, mine, kept,
    to_partner, from_partner, to_peer, from_peer, chol, table_sem, chol_sem,
    partner_send, partner_recv, peer_send, peer_recv, *sems
):
    gather = Gather(row_count, col_count, pieces, own, rows, held, sems, direct=True)
    me_row, depth = gather.me_row, gather.depth
    partner = me_row + 1 - 2 * lax.rem(me_row, 2)
    half = row_count // 2
    split = table_sem.shape[0]
    chunk = table.shape[0] // split
    tile = min(512, table.shape[1])
    tiles = table.shape[1] // tile

    def table_copy(index):
        span = pl.ds(index * chunk, chunk)
        return pltpu.make_async_copy(
            amplitudes.at[span, :], table.at[span, :], table_sem.at[index]
        )

    def chol_copy(piece):
        return pltpu.make_async_copy(
            own.at[gather.part(piece), :], chol.at[piece], chol_sem.at[piece]
        )

    def partner_copy(piece):
        return pltpu.make_async_remote_copy(
            src_ref=to_partner.at[piece % 2],
            dst_ref=from_partner.at[piece],
            send_sem=partner_send.at[piece],
            recv_sem=partner_recv.at[piece],
            device_id={"row": partner},
            device_id_type=MESH,
        )

    def peer_copy(step, piece):
        return pltpu.make_async_remote_copy(
            src_ref=to_peer.at[piece % 2, step - 1],
            dst_ref=from_peer.at[piece, half - step - 1],
            send_sem=peer_send.at[piece, step],
            recv_sem=peer_recv.at[piece, half - step],
            device_id={"row": lax.rem(me_row + 2 * step, row_count)},
            device_id_type=MESH,
        )

    def multiply(piece):
        if piece >= 2:
            partner_copy(piece - 2).wait_send()

        @pl.loop(0, tiles)
        def _(index):
            span = pl.ds(pl.multiple_of(index * tile, tile), tile)
            product = jnp.dot(
                rows[piece], table[:, span], preferred_element_type=jnp.float32
            )
            mine[:, span] = product[: half * depth]
            to_partner[piece % 2, :, span] = product[half * depth :].astype(jnp.bfloat16)

        partner_copy(piece).start()

    def pair(piece):
        partner_copy(piece).wait_recv()
        if piece >= 2:
            for step in range(1, half):
                peer_copy(step, piece - 2).wait_send()

        @pl.loop(0, tiles)
        def _(index):
            span = pl.ds(pl.multiple_of(index * tile, tile), tile)
            both = mine[:, span] + from_partner[piece, :, span].astype(jnp.float32)
            kept[piece % 2, :, span] = both[:depth]
            for step in range(1, half):
                to_peer[piece % 2, step - 1, :, span] = both[
                    step * depth : (step + 1) * depth
                ].astype(jnp.bfloat16)

        for step in range(1, half):
            peer_copy(step, piece).start()

    def close(piece):
        chol_copy(piece).wait()
        for step in range(1, half):
            peer_copy(step, piece).wait_recv()

        @pl.loop(0, tiles)
        def _(index):
            span = pl.ds(pl.multiple_of(index * tile, tile), tile)
            total = kept[piece % 2, :, span]
            for step in range(1, half):
                total = total + from_peer[piece, step - 1, :, span].astype(jnp.float32)
            total = chol[piece, :, span].astype(jnp.float32) + total
            dressed[gather.part(piece), span] = total.astype(jnp.bfloat16)

    enter(row_count, col_count, gather.me_row, gather.me_col)
    for piece in range(min(2, pieces)):
        gather.begin(piece)
    for index in range(split):
        table_copy(index).start()
    for piece in range(pieces):
        chol_copy(piece).start()
    for step in range(pieces + col_count):
        if step + 2 < pieces:
            gather.begin(step + 2)
        for hops in range(1, col_count):
            if 0 <= step - hops + 1 < pieces:
                gather.arrive(hops, step - hops + 1)
        piece = step - (col_count - 2)
        if 0 <= piece - 1 < pieces:
            pair(piece - 1)
        if 0 <= piece - 2 < pieces:
            close(piece - 2)
        if 0 <= piece < pieces:
            gather.wait_rows(piece)
            if piece == 0:
                for index in range(split):
                    table_copy(index).wait()
            multiply(piece)
    for piece in range(pieces):
        gather.wait_sends(piece)
        if piece >= pieces - 2:
            partner_copy(piece).wait_send()
            for step in range(1, half):
                peer_copy(step, piece).wait_send()


def dress_pairs(amplitudes, own, row_count, col_count, collective_id):
    depth, width = own.shape
    pieces = max(1, min(4, depth // 16))
    depth_piece, half = depth // pieces, row_count // 2
    bf16, f32, dma = jnp.bfloat16, jnp.float32, pltpu.SemaphoreType.DMA
    scratch = [
        pltpu.VMEM(amplitudes.shape, bf16),
        pltpu.VMEM((pieces, row_count * depth_piece, amplitudes.shape[0]), bf16),
        pltpu.VMEM((half * depth_piece, width), f32),
        pltpu.VMEM((2, depth_piece, width), f32),
        pltpu.VMEM((2, half * depth_piece, width), bf16),
        pltpu.VMEM((pieces, half * depth_piece, width), bf16),
        pltpu.VMEM((2, half - 1, depth_piece, width), bf16),
        pltpu.VMEM((pieces, half - 1, depth_piece, width), bf16),
        pltpu.VMEM((pieces, depth_piece, width), bf16),
        dma((4,)),
        dma((pieces,)),
        dma((pieces,)),
        dma((pieces,)),
        dma((pieces, half)),
        dma((pieces, half)),
    ] + gather_sems(row_count, col_count, pieces)
    _, dressed = pl.pallas_call(
        functools.partial(dress_kernel, row_count, col_count, pieces),
        out_shape=(
            jax.ShapeDtypeStruct((col_count, depth, width), bf16),
            jax.ShapeDtypeStruct((depth, width), bf16),
        ),
        in_specs=[pl.BlockSpec(memory_space=pl.ANY)] * 2,
        out_specs=(
            pl.BlockSpec(memory_space=pl.ANY),
            pl.BlockSpec(memory_space=pltpu.VMEM),
        ),
        scratch_shapes=scratch,
        compiler_params=pltpu.CompilerParams(
            collective_id=collective_id, has_side_effects=True, vmem_limit_bytes=67043328
        ),
        name="dress",
    )(amplitudes, own)
    return dressed


def local(row_count, col_count, amplitudes, cholesky, occ_index, vir_index, eps_occ, eps_vir):
    row_position = lax.axis_index("row")
    col_position = lax.axis_index("col")
    rows_block, cols_block = amplitudes.shape
    ydress = dress_pairs(amplitudes, cholesky, row_count, col_count, 0)
    contract = (((0,), (0,)), ((), ()))
    ydress_rows, ydress_cols = gather_pairs(ydress, row_count, col_count, True, 1)
    gram = lax.dot_general(
        ydress_rows, ydress_cols, contract, preferred_element_type=jnp.float32
    )
    gap_rows = pair_gaps(
        occ_index, vir_index, eps_occ, eps_vir, row_position * rows_block, rows_block
    )
    gap_cols = pair_gaps(
        occ_index, vir_index, eps_occ, eps_vir, col_position * cols_block, cols_block
    )
    return (-gram / (gap_rows[:, None] + gap_cols[None, :])).astype(jnp.bfloat16)


def solution(mesh):
    return jax.shard_map(
        functools.partial(local, mesh.shape["row"], mesh.shape["col"]),
        mesh=mesh,
        in_specs=(
            P(("grp", "row"), "col"),
            P("row", ("grp", "col")),
            P("grp"),
            P("grp"),
            P("grp"),
            P("grp"),
        ),
        out_specs=P(("grp", "row"), "col"),
        check_vma=False,
    )
```

```python
import functools

import jax
import jax.numpy as jnp
from jax import lax
from jax.experimental import pallas as pl
from jax.experimental.pallas import tpu as pltpu
from jax.sharding import PartitionSpec as P

MESH = pl.DeviceIdType.MESH


def pair_gaps(occ_index, vir_index, eps_occ, eps_vir, begin_pair, pair_count):
    occ_rows = lax.dynamic_slice_in_dim(occ_index, begin_pair, pair_count, 0)
    vir_rows = lax.dynamic_slice_in_dim(vir_index, begin_pair, pair_count, 0)
    occ_table = jnp.arange(eps_occ.shape[0], dtype=jnp.int32)
    vir_table = jnp.arange(eps_vir.shape[0], dtype=jnp.int32)
    occ_energy = jnp.sum(
        jnp.where(occ_rows[:, None] == occ_table[None, :], eps_occ[None, :], 0.0), axis=1
    )
    vir_energy = jnp.sum(
        jnp.where(vir_rows[:, None] == vir_table[None, :], eps_vir[None, :], 0.0), axis=1
    )
    return vir_energy - occ_energy


def enter(row_count, col_count, me_row, me_col):
    barrier = pltpu.get_barrier_semaphore()
    for step in range(1, row_count):
        pl.semaphore_signal(
            barrier,
            inc=1,
            device_id={"row": lax.rem(me_row + step, row_count)},
            device_id_type=MESH,
        )
    for condition, where in ((me_col > 0, -1), (me_col < col_count - 1, 1)):

        @pl.when(condition)
        def _():
            pl.semaphore_signal(
                barrier, inc=1, device_id={"col": me_col + where}, device_id_type=MESH
            )

    neighbours = jnp.minimum(me_col, 1) + jnp.minimum(col_count - 1 - me_col, 1)
    pl.semaphore_wait(barrier, row_count - 1 + neighbours)


class Gather:
    def __init__(self, row_count, col_count, pieces, own, rows, held, sems, packed):
        self.packed = packed
        self.row_count, self.col_count, self.pieces = row_count, col_count, pieces
        self.own, self.rows, self.held = own, rows, held
        self.send_line, self.recv_line, self.send_row, self.recv_row, self.keep = sems
        self.me_row, self.me_col = lax.axis_index("row"), lax.axis_index("col")
        self.depth = own.shape[0] // pieces
        self.share = row_count // col_count
        self.width = own.shape[1] // self.share

    def part(self, piece):
        return pl.ds(piece * self.depth, self.depth)

    def block_ref(self, block, piece, mine):
        if mine:
            return self.own.at[self.part(piece), :]
        return self.held.at[block, self.part(piece), :]

    def block_part(self, block, index, piece, mine):
        columns = pl.ds(index * self.width, self.width)
        if mine:
            return self.own.at[self.part(piece), columns]
        return self.held.at[block, self.part(piece), columns]

    def row_ref(self, owner, target, piece):
        if not self.packed:
            return self.rows.at[owner, self.part(piece), :]
        half = self.row_count // 2
        other = lax.rem(owner + target, 2)
        base = target + other * (1 - 2 * lax.rem(target, 2))
        slot = lax.rem(owner - base + self.row_count, self.row_count) // 2 + other * half
        begin = pl.multiple_of(slot * self.depth, self.depth)
        return self.rows.at[piece, pl.ds(begin, self.depth), :]

    def line_copy(self, side, block, hops, piece):
        return pltpu.make_async_remote_copy(
            src_ref=self.block_ref(block, piece, hops == 0),
            dst_ref=self.held.at[block, self.part(piece), :],
            send_sem=self.send_line.at[side, hops, piece],
            recv_sem=self.recv_line.at[side, hops, piece],
            device_id={"col": self.me_col + (1 if side == 0 else -1)},
            device_id_type=MESH,
        )

    def row_copy(self, block, index, piece, mine=False):
        return pltpu.make_async_remote_copy(
            src_ref=self.block_part(block, index, piece, mine),
            dst_ref=self.row_ref(self.me_row, block * self.share + index, piece),
            send_sem=self.send_row.at[block, index, piece],
            recv_sem=self.recv_row.at[self.me_row, piece],
            device_id={"row": block * self.share + index},
            device_id_type=MESH,
        )

    def keep_copy(self, block, index, piece, mine=False):
        return pltpu.make_async_copy(
            self.block_part(block, index, piece, mine),
            self.row_ref(self.me_row, self.me_row, piece),
            self.keep.at[piece],
        )

    def on(self, side):
        return self.me_col < self.col_count - 1 if side == 0 else self.me_col > 0

    def spread(self, block, piece, mine=False):
        for index in range(self.share):
            target = block * self.share + index

            @pl.when(target == self.me_row)
            def _():
                self.keep_copy(block, index, piece, mine).start()

            @pl.when(target != self.me_row)
            def _():
                self.row_copy(block, index, piece, mine).start()

    def begin(self, piece):
        for side in range(2):

            @pl.when(self.on(side))
            def _():
                self.line_copy(side, self.me_col, 0, piece).start()

        self.spread(self.me_col, piece, True)

    def source(self, side, hops):
        block = self.me_col - hops if side == 0 else self.me_col + hops
        exists = self.me_col >= hops if side == 0 else self.me_col + hops < self.col_count
        return block, exists

    def arrive(self, hops, piece):
        for side in range(2):
            block, exists = self.source(side, hops)

            @pl.when(exists)
            def _():
                self.line_copy(side, block, hops - 1, piece).wait_recv()

                if hops < self.col_count - 1:

                    @pl.when(self.on(side))
                    def _():
                        self.line_copy(side, block, hops, piece).start()

                self.spread(block, piece)

    def wait_rows(self, piece):
        for other in range(self.row_count):

            @pl.when(other != self.me_row)
            def _():
                pltpu.make_async_remote_copy(
                    src_ref=self.row_ref(other, self.me_row, piece),
                    dst_ref=self.row_ref(other, self.me_row, piece),
                    send_sem=self.send_row.at[0, 0, piece],
                    recv_sem=self.recv_row.at[other, piece],
                    device_id={"row": other},
                    device_id_type=MESH,
                ).wait_recv()

        for block in range(self.col_count):
            for index in range(self.share):

                @pl.when(block * self.share + index == self.me_row)
                def _():
                    self.keep_copy(block, index, piece).wait()

    def wait_sends(self, piece):
        for side in range(2):
            for hops in range(self.col_count - 1):
                block, exists = self.source(side, hops)

                @pl.when(jnp.logical_and(exists, self.on(side)))
                def _():
                    self.line_copy(side, block, hops, piece).wait_send()

        for block in range(self.col_count):
            for index in range(self.share):

                @pl.when(block * self.share + index != self.me_row)
                def _():
                    self.row_copy(block, index, piece).wait_send()


def gather_sems(row_count, col_count, pieces):
    return [
        pltpu.SemaphoreType.DMA((2, col_count, pieces)),
        pltpu.SemaphoreType.DMA((2, col_count, pieces)),
        pltpu.SemaphoreType.DMA((col_count, row_count // col_count, pieces)),
        pltpu.SemaphoreType.DMA((row_count, pieces)),
        pltpu.SemaphoreType.DMA((pieces,)),
    ]


class Columns:
    def __init__(self, row_count, pieces, own, cols, sems):
        self.row_count, self.pieces, self.own, self.cols = row_count, pieces, own, cols
        self.load, self.send, self.recv, self.send_on = sems
        self.me_row = lax.axis_index("row")
        self.partner = self.me_row + 1 - 2 * lax.rem(self.me_row, 2)
        self.depth = own.shape[0] // pieces

    def part(self, piece):
        return pl.ds(piece * self.depth, self.depth)

    def copy(self, owner, target, sem, piece, src=None):
        dst = self.cols.at[owner, self.part(piece), :]
        return pltpu.make_async_remote_copy(
            src_ref=dst if src is None else src,
            dst_ref=dst,
            send_sem=sem,
            recv_sem=self.recv.at[owner, piece],
            device_id={"row": target},
            device_id_type=MESH,
        )

    def peers(self):
        peers = [(0, self.partner)]
        for step in range(1, self.row_count // 2):
            peers.append((step, lax.rem(self.me_row + 2 * step, self.row_count)))
        return peers

    def first(self, slot, target, piece, src):
        return self.copy(self.me_row, target, self.send.at[slot, piece], piece, src)

    def begin(self, piece, src):
        for slot, target in self.peers():
            self.first(slot, target, piece, src).start()

    def arrive(self, piece):
        for slot, owner in self.peers()[1:]:
            self.copy(owner, self.partner, self.send_on.at[slot, piece], piece).wait_recv()
            self.copy(owner, self.partner, self.send_on.at[slot, piece], piece).start()

    def finish(self, piece, src):
        for slot, target in self.peers():
            self.first(slot, target, piece, src).wait_send()
        self.copy(self.partner, self.partner, self.send.at[0, piece], piece).wait_recv()
        for slot, owner in self.peers()[1:]:
            self.copy(owner, self.partner, self.send_on.at[slot, piece], piece).wait_send()
            theirs = lax.rem(self.partner + 2 * slot, self.row_count)
            self.copy(theirs, self.partner, self.send.at[0, piece], piece).wait_recv()


def columns_sems(row_count, pieces):
    return [
        pltpu.SemaphoreType.DMA((pieces,)),
        pltpu.SemaphoreType.DMA((row_count // 2, pieces)),
        pltpu.SemaphoreType.DMA((row_count, pieces)),
        pltpu.SemaphoreType.DMA((row_count // 2, pieces)),
    ]


def dress_kernel(
    row_count, col_count, pieces, amplitudes, own, held, held_y, y_rows, y_cols, dressed, table, rows, mine, kept,
    to_partner, from_partner, to_peer, from_peer, chol, table_sem, chol_sem,
    partner_send, partner_recv, peer_send, peer_recv, *sems
):
    gather = Gather(row_count, col_count, pieces, own, rows, held, sems[:5], True)
    second = Gather(
        row_count, col_count, pieces, dressed, y_rows, held_y, sems[5:10], False
    )
    columns = Columns(row_count, pieces, dressed, y_cols, sems[10:])
    me_row, depth = gather.me_row, gather.depth
    partner = me_row + 1 - 2 * lax.rem(me_row, 2)
    half = row_count // 2
    split = table_sem.shape[0]
    chunk = table.shape[0] // split
    tile = min(512, table.shape[1])
    tiles = table.shape[1] // tile

    def table_copy(index):
        span = pl.ds(index * chunk, chunk)
        return pltpu.make_async_copy(
            amplitudes.at[span, :], table.at[span, :], table_sem.at[index]
        )

    def chol_copy(piece):
        return pltpu.make_async_copy(
            own.at[gather.part(piece), :], chol.at[piece], chol_sem.at[piece]
        )

    def partner_copy(piece):
        return pltpu.make_async_remote_copy(
            src_ref=to_partner.at[piece % 2],
            dst_ref=from_partner.at[piece],
            send_sem=partner_send.at[piece],
            recv_sem=partner_recv.at[piece],
            device_id={"row": partner},
            device_id_type=MESH,
        )

    def peer_copy(step, piece):
        return pltpu.make_async_remote_copy(
            src_ref=to_peer.at[piece % 2, step - 1],
            dst_ref=from_peer.at[piece, half - step - 1],
            send_sem=peer_send.at[piece, step],
            recv_sem=peer_recv.at[piece, half - step],
            device_id={"row": lax.rem(me_row + 2 * step, row_count)},
            device_id_type=MESH,
        )

    def multiply(piece):
        if piece >= 2:
            partner_copy(piece - 2).wait_send()

        @pl.loop(0, tiles)
        def _(index):
            span = pl.ds(pl.multiple_of(index * tile, tile), tile)
            product = jnp.dot(
                rows[piece], table[:, span], preferred_element_type=jnp.float32
            )
            mine[:, span] = product[: half * depth]
            to_partner[piece % 2, :, span] = product[half * depth :].astype(jnp.bfloat16)

        partner_copy(piece).start()

    def pair(piece):
        partner_copy(piece).wait_recv()
        if piece >= 2:
            for step in range(1, half):
                peer_copy(step, piece - 2).wait_send()

        @pl.loop(0, tiles)
        def _(index):
            span = pl.ds(pl.multiple_of(index * tile, tile), tile)
            both = mine[:, span] + from_partner[piece, :, span].astype(jnp.float32)
            kept[piece % 2, :, span] = both[:depth]
            for step in range(1, half):
                to_peer[piece % 2, step - 1, :, span] = both[
                    step * depth : (step + 1) * depth
                ].astype(jnp.bfloat16)

        for step in range(1, half):
            peer_copy(step, piece).start()

    def close(piece):
        chol_copy(piece).wait()
        for step in range(1, half):
            peer_copy(step, piece).wait_recv()

        @pl.loop(0, tiles)
        def _(index):
            span = pl.ds(pl.multiple_of(index * tile, tile), tile)
            total = kept[piece % 2, :, span]
            for step in range(1, half):
                total = total + from_peer[piece, step - 1, :, span].astype(jnp.float32)
            total = chol[piece, :, span].astype(jnp.float32) + total
            dressed[gather.part(piece), span] = total.astype(jnp.bfloat16)

    def own_y(piece):
        return dressed.at[gather.part(piece), :]

    def own_cols(piece):
        return pltpu.make_async_copy(
            own_y(piece), y_cols.at[me_row, gather.part(piece), :], columns.load.at[piece]
        )

    enter(row_count, col_count, gather.me_row, gather.me_col)
    for piece in range(min(2, pieces)):
        gather.begin(piece)
    for index in range(split):
        table_copy(index).start()
    for piece in range(pieces):
        chol_copy(piece).start()
    for step in range(pieces + 2 * col_count - 1):
        if step + 2 < pieces:
            gather.begin(step + 2)
        for hops in range(1, col_count):
            if 0 <= step - hops + 1 < pieces:
                gather.arrive(hops, step - hops + 1)
        piece = step - (col_count - 2)
        if 0 <= piece - 1 < pieces:
            pair(piece - 1)
        if 0 <= piece - 2 < pieces:
            close(piece - 2)
            second.begin(piece - 2)
            own_cols(piece - 2).start()
            columns.begin(piece - 2, own_y(piece - 2))
        if 0 <= piece < pieces:
            gather.wait_rows(piece)
            if piece == 0:
                for index in range(split):
                    table_copy(index).wait()
            multiply(piece)
        for hops in range(1, col_count):
            if 0 <= step - col_count - hops < pieces:
                second.arrive(hops, step - col_count - hops)
        if 0 <= step - col_count - 1 < pieces:
            columns.arrive(step - col_count - 1)
    for piece in range(pieces):
        gather.wait_sends(piece)
        second.wait_rows(piece)
        second.wait_sends(piece)
        own_cols(piece).wait()
        columns.finish(piece, own_y(piece))
        if piece >= pieces - 2:
            partner_copy(piece).wait_send()
            for step in range(1, half):
                peer_copy(step, piece).wait_send()


def dress_pairs(amplitudes, own, row_count, col_count, collective_id):
    depth, width = own.shape
    pieces = max(1, min(4, depth // 16))
    depth_piece, half = depth // pieces, row_count // 2
    bf16, f32, dma = jnp.bfloat16, jnp.float32, pltpu.SemaphoreType.DMA
    scratch = [
        pltpu.VMEM((depth, width), bf16),
        pltpu.VMEM(amplitudes.shape, bf16),
        pltpu.VMEM((pieces, row_count * depth_piece, amplitudes.shape[0]), bf16),
        pltpu.VMEM((half * depth_piece, width), f32),
        pltpu.VMEM((2, depth_piece, width), f32),
        pltpu.VMEM((2, half * depth_piece, width), bf16),
        pltpu.VMEM((pieces, half * depth_piece, width), bf16),
        pltpu.VMEM((2, half - 1, depth_piece, width), bf16),
        pltpu.VMEM((pieces, half - 1, depth_piece, width), bf16),
        pltpu.VMEM((pieces, depth_piece, width), bf16),
        dma((4,)),
        dma((pieces,)),
        dma((pieces,)),
        dma((pieces,)),
        dma((pieces, half)),
        dma((pieces, half)),
    ]
    scratch += gather_sems(row_count, col_count, pieces) * 2 + columns_sems(row_count, pieces)
    rows_width = amplitudes.shape[0]
    _, _, y_rows, y_cols = pl.pallas_call(
        functools.partial(dress_kernel, row_count, col_count, pieces),
        out_shape=(
            jax.ShapeDtypeStruct((col_count, depth, width), bf16),
            jax.ShapeDtypeStruct((col_count, depth, width), bf16),
            jax.ShapeDtypeStruct((row_count, depth, rows_width), bf16),
            jax.ShapeDtypeStruct((row_count, depth, width), bf16),
        ),
        in_specs=[pl.BlockSpec(memory_space=pl.ANY)] * 2,
        out_specs=(pl.BlockSpec(memory_space=pl.ANY),) * 4,
        scratch_shapes=scratch,
        compiler_params=pltpu.CompilerParams(
            collective_id=collective_id, has_side_effects=True, vmem_limit_bytes=67043328
        ),
        name="dress",
    )(amplitudes, own)
    return (
        y_rows.reshape(row_count * depth, rows_width),
        y_cols.reshape(row_count * depth, width),
    )


def local(row_count, col_count, amplitudes, cholesky, occ_index, vir_index, eps_occ, eps_vir):
    row_position = lax.axis_index("row")
    col_position = lax.axis_index("col")
    rows_block, cols_block = amplitudes.shape
    ydress_rows, ydress_cols = dress_pairs(amplitudes, cholesky, row_count, col_count, 0)
    contract = (((0,), (0,)), ((), ()))
    gram = lax.dot_general(
        ydress_rows, ydress_cols, contract, preferred_element_type=jnp.float32
    )
    gap_rows = pair_gaps(
        occ_index, vir_index, eps_occ, eps_vir, row_position * rows_block, rows_block
    )
    gap_cols = pair_gaps(
        occ_index, vir_index, eps_occ, eps_vir, col_position * cols_block, cols_block
    )
    return (-gram / (gap_rows[:, None] + gap_cols[None, :])).astype(jnp.bfloat16)


def solution(mesh):
    return jax.shard_map(
        functools.partial(local, mesh.shape["row"], mesh.shape["col"]),
        mesh=mesh,
        in_specs=(
            P(("grp", "row"), "col"),
            P("row", ("grp", "col")),
            P("grp"),
            P("grp"),
            P("grp"),
            P("grp"),
        ),
        out_specs=P(("grp", "row"), "col"),
        check_vma=False,
    )
```
